32 devices in a mesh: gx: 2 (over y), gy: 4 (over x, core), gz: 4 (over z).
Axes of the slice: x: 2, y: 2, z: 4, core: 2. Of those that a mesh axis runs over, the one named last changes fastest.
Arguments:
- snapshot: float32 [12, 1024, 8, 512], P(None, 'gz', 'gx', 'gy'), may hold values from -108 to 108
- species_pick: int32 [8], replicated, may hold values from 0 to 11, as said below
- basis_start: float32 [1024, 384], replicated, may hold values from -0.1875 to 0.1875
Outputs:
- gram_matrix: float32 [1024, 1024], P(('gx', 'gy', 'gz'))
- basis: float32 [1024, 384], P(('gx', 'gy', 'gz'))
- core_tensor: float32 [8, 384, 8, 512], P(None, None, ('gx', 'gz'), 'gy')
The draws below stay inside these ranges and needn't reach their ends.
Inputs may be any that keep to these rules, and one draw needn't show every extreme that they name: `species_pick`: 8 distinct species numbers; 0 and 11 are always among them.
All inputs are finite; a program needn't handle non-finite values.
Results may differ from the reference program's by a relative error of at most 0.0003.
Values sent between devices are 32-bit elements; how exact they have to be, the bound alone decides.
A program may use at most 128 MiB of HBM per device.

```python
import math
import jax
import jax.numpy as jnp
from jax import lax

NX = 1024
RANK = 384
NSTORE = 12
S = 8
NY = 8
NZ = 512


def draw_snapshot(key, part):
    keys = jax.random.split(key, 4)
    shape = (NSTORE, NX, NY, NZ)
    noise = jnp.clip(jax.random.normal(keys[0], shape, jnp.float32), -6.0, 6.0)
    row_scale = jnp.exp(jax.random.uniform(keys[1], (NX,), jnp.float32, math.log(0.3), math.log(3.0)))
    species_scale = jnp.exp(jax.random.uniform(keys[2], (NSTORE,), jnp.float32, math.log(0.5), math.log(2.0)))
    cell_scale = jnp.exp(jax.random.uniform(keys[3], (NY, NZ), jnp.float32, math.log(0.3), math.log(3.0)))
    return noise * species_scale[:, None, None, None] * row_scale[None, :, None, None] * cell_scale[None, None, :, :]


def draw_species_pick(key, part):
    inner_pick = jax.random.permutation(jax.random.fold_in(key, 11), NSTORE - 2)[:S - 2] + 1
    ends = jnp.array([0, NSTORE - 1], jnp.int32)
    chosen = jnp.concatenate([ends, inner_pick.astype(jnp.int32)])
    return jax.random.permutation(jax.random.fold_in(key, 12), chosen).astype(jnp.int32)


def bell_draw(rng, extent, scale, limit, dtype=jnp.bfloat16):
    return jnp.clip(scale * jax.random.normal(rng, extent, jnp.float32), -limit, limit).astype(dtype)


def setup_inputs(seed: int = 0) -> dict:
    key_of = jax.random.split(jax.random.key(seed), 4)
    return {
        "snapshot": draw_snapshot(jax.random.fold_in(key_of[3], 71), 0),
        "species_pick": draw_species_pick(jax.random.fold_in(key_of[3], 71), 0),
        "basis_start": bell_draw(key_of[2], (NX, RANK), NX ** -0.5, 0.1875, jnp.float32),
    }


def reference(snapshot, species_pick, basis_start):
    highest = lax.Precision.HIGHEST

    def accumulate(position, total):
        chosen = lax.dynamic_index_in_dim(snapshot, species_pick[position], 0, keepdims=False)
        columns = chosen.reshape(NX, NY * NZ)
        return total + jnp.dot(columns.astype(jnp.float32), columns.T.astype(jnp.float32), precision=highest, preferred_element_type=jnp.float32)
    gram_total = lax.fori_loop(0, S, accumulate, jnp.zeros((NX, NX), jnp.float32))
    gram_matrix = gram_total / (S * NY * NZ)
    image_full = jnp.dot(gram_matrix, basis_start, precision=highest)
    inner_gram = jnp.dot(image_full.T, image_full, precision=highest)
    lower_factor = jnp.linalg.cholesky(inner_gram)
    basis = jax.scipy.linalg.solve_triangular(lower_factor, image_full.T, lower=True).T

    def project(species_index):
        chosen = lax.dynamic_index_in_dim(snapshot, species_index, 0, keepdims=False)
        return jnp.einsum('xr,xyz->ryz', basis, chosen, precision=highest)
    core_tensor = lax.map(project, species_pick)
    return (gram_matrix, basis, core_tensor)
```

```python
import functools

import jax
import jax.numpy as jnp
from jax import lax
from jax.experimental import pallas as pl
from jax.experimental.pallas import tpu as pltpu
from jax.sharding import PartitionSpec as P

HIGHEST = lax.Precision.HIGHEST
F32 = jnp.float32
BF16 = jnp.bfloat16
BLOCK = 128
TILE = 8


def split(x):
    high = x.astype(BF16)
    return high, (x - high.astype(F32)).astype(BF16)


def dot(a, b, contract, precision=None):
    return lax.dot_general(
        a, b, (((contract[0],), (contract[1],)), ((), ())),
        precision=precision, preferred_element_type=F32,
    )


def eliminate(read):
    count = BLOCK // TILE
    row = lax.broadcasted_iota(jnp.int32, (TILE, BLOCK), 0)
    lane = lax.broadcasted_iota(jnp.int32, (TILE, BLOCK), 1)
    left = [read(i) for i in range(count)]
    right = [(lane == row + TILE * i).astype(F32) for i in range(count)]

    def wide(x):
        return jnp.broadcast_to(x, (TILE, BLOCK))

    for t in range(count):
        columns = [wide(left[t][:, TILE * t + l:TILE * t + l + 1]) for l in range(TILE)]
        pivots, inverses, upper, lrows, rrows = [], [], [], [], []
        for l in range(TILE):
            pivot = wide(columns[l][l:l + 1, :])
            inverse = 1.0 / pivot
            factor = jnp.where(row > l, columns[l] * inverse, 0.0)
            lrow, rrow = wide(left[t][l:l + 1, :]), wide(right[t][l:l + 1, :])
            ahead = {}
            for m in range(l + 1, TILE):
                ahead[m] = wide(columns[m][l:l + 1, :])
                columns[m] = columns[m] - factor * ahead[m]
            left[t] = left[t] - factor * lrow
            right[t] = right[t] - factor * rrow
            pivots.append(pivot)
            inverses.append(inverse)
            upper.append(ahead)
            lrows.append(lrow)
            rrows.append(rrow)
        for i in range(t + 1, count):
            below = [wide(left[i][:, TILE * t + l:TILE * t + l + 1]) for l in range(TILE)]
            for l in range(TILE):
                factor = below[l] * inverses[l]
                for m in range(l + 1, TILE):
                    below[m] = below[m] - factor * upper[l][m]
                left[i] = left[i] - factor * lrows[l]
                right[i] = right[i] - factor * rrows[l]
        diagonal = pivots[0]
        for l in range(1, TILE):
            diagonal = jnp.where(row == l, pivots[l], diagonal)
        scale = lax.rsqrt(diagonal)
        scale = scale * (1.5 - 0.5 * diagonal * scale * scale)
        right[t] = right[t] * scale
    return right


def hdot(a, b, contract):
    return dot(a, b, contract, HIGHEST)


def dot3(a, b, contract):
    (ah, al), (bh, bl) = a, b
    return dot(ah, bh, contract) + (dot(ah, bl, contract) + dot(al, bh, contract))


def chunked(species):
    sizes = [2] * ((species - 2) // 2) + [1] * (species - (species - 2) // 2 * 2)
    chunks, first = [], 0
    for size in sizes:
        chunks.append(range(first, first + size))
        first += size
    return chunks


def main_kernel(dims, scaling, pick_ref, snap_ref, start_ref, gram_ref, basis_ref, core_ref,
                snap, outgoing, panel, start, xh, xl, bh, bl, wh, wl, gram, image,
                r0, s1, r1, s2, r2, im, g0, gs, g1, gt, g2, a_ref, w_ref, u_ref, y_ref,
                load_sem, own_sem, send, recv):
    nx, nh, nl, nz = dims
    plane = nx * nh
    gx, gy, gz = lax.axis_index("gx"), lax.axis_index("gy"), lax.axis_index("gz")
    yh, yl = gy // nl, gy % nl
    me = gx * nh + yh
    stored = snap.shape[0]
    _, species, rows, width = outgoing.shape
    total, rank = start.shape
    blocks = rank // BLOCK
    quarters, gram_width = gram.shape[0], gram.shape[3]
    share = im.shape[4]
    group = nz * share
    tall = rows // (nl * group)
    chunks = chunked(species)
    peers = {
        "p": [(p, {"gx": p // nh, "gy": p % nh * nl + yl})
              for p in [(me + k) % plane for k in range(1, plane)]],
        "l": [(p, {"gy": yh * nl + p}) for p in [(yl + k) % nl for k in range(1, nl)]],
        "z": [(p, {"gz": p}) for p in [(gz + k) % nz for k in range(1, nz)]],
    }
    started = []

    def exchange(key, source, target):
        copies = []
        for k, (p, place) in enumerate(peers[key]):
            i = len(started)
            copy = pltpu.make_async_remote_copy(
                src_ref=source(p), dst_ref=target(k), send_sem=send.at[i], recv_sem=recv.at[i],
                device_id=place, device_id_type=pl.DeviceIdType.MESH,
            )
            copy.start()
            copies.append(copy)
            started.append(copy)
        return copies

    def arrived(copies):
        for copy in copies:
            copy.wait_recv()

    def part(p, size):
        return pl.ds(pl.multiple_of(p * size, size), size)

    def plus(first, buffer, count):
        for k in range(count):
            first = first + buffer(k)
        return first

    loads = [pltpu.make_async_copy(snap_ref.at[s], snap.at[s], load_sem.at[s]) for s in range(stored)]
    loads.append(pltpu.make_async_copy(start_ref, start, load_sem.at[stored]))
    for load in loads:
        load.start()
    barrier = pltpu.get_barrier_semaphore()
    count = 0
    for key in "zpl":
        for p, place in peers[key]:
            pl.semaphore_signal(barrier, inc=1, device_id=place, device_id_type=pl.DeviceIdType.MESH)
            count += 1
    for load in loads[:-1]:
        load.wait()

    landing = []
    for j, members in enumerate(chunks):
        for s in members:
            for p in range(nz):
                outgoing[p, s] = snap[pick_ref[s], pl.ds(p, rows, stride=nz), :]
        if j == 0:
            pl.semaphore_wait(barrier, count)
        these = pl.ds(members[0], len(members))
        copies = exchange("z", lambda p: outgoing.at[p, these], lambda k: panel.at[these, gz])
        own = pltpu.make_async_copy(outgoing.at[gz, these], panel.at[these, gz], own_sem.at[j])
        own.start()
        landing.append((copies, own))

    loads[-1].wait()
    bh[...], bl[...] = split(start[...])

    def columns(members):
        return slice(members[0] * width, (members[-1] + 1) * width)

    def add_image(j, members):
        copies, own = landing[j]
        own.wait()
        arrived(copies)
        for s in members:
            upper, lower = split(panel[s].reshape(total, width))
            xh[:, s * width:(s + 1) * width] = upper
            xl[:, s * width:(s + 1) * width] = lower
        cut = columns(members)
        n = len(members) * width
        w = dot3((xh[:, cut], xl[:, cut]), (bh[...], bl[...]), (0, 0)) * scaling
        wh[0:n, :], wl[0:n, :] = split(w)

        @pl.loop(0, total // rows)
        def _(a):
            here = part(a, rows)
            term = dot3((xh[here, cut], xl[here, cut]), (wh[0:n, :], wl[0:n, :]), (1, 0))
            there = pl.ds(a * tall, tall)
            for c in range(blocks):
                block = term[:, c * BLOCK:(c + 1) * BLOCK].reshape(tall, nl * group, BLOCK)
                image[c, there] = block if j == 0 else image[c, there] + block

    def add_gram(j, members):
        cut = columns(members)

        @pl.loop(0, total // rows)
        def _(a):
            here = part(a, rows)
            there = pl.ds(a * tall, tall)
            ah, al = xh[here, cut], xl[here, cut]
            for b in range(quarters):
                that = slice(b * gram_width, (b + 1) * gram_width)
                term = dot3((ah, al), (xh[that, cut], xl[that, cut]), (1, 1))
                term = term.reshape(tall, nl * group, gram_width)
                if j > 0:
                    term = term + gram[b, there]
                if j == len(chunks) - 1:
                    term = term * scaling
                gram[b, there] = term

    for j, members in enumerate(chunks):
        add_image(j, members)
        if j < len(chunks) - 1:
            add_gram(j, members)

    every = range(blocks)
    two = [exchange("l", lambda p: image.at[c, :, part(p, group)], lambda k: r0.at[c, k]) for c in every]
    add_gram(len(chunks) - 1, chunks[-1])
    gram_two = [exchange("l", lambda p: gram.at[q, :, part(p, group)], lambda k: g0.at[q, k])
                for q in range(quarters)]
    flat = []
    for c in every:
        arrived(two[c])
        s1[c] = plus(image[c, :, part(yl, group)], lambda k: r0[c, k], nl - 1)
        flat.append(exchange("p", lambda p: s1.at[c, p], lambda k: r1.at[c, k]))
    line = []
    for c in every:
        arrived(flat[c])
        s2[c] = plus(s1[c, me], lambda k: r1[c, k], plane - 1)
        line.append(exchange("z", lambda p: s2.at[c, part(p, share)], lambda k: r2.at[c, k]))
    line_back = []
    for c in every:
        arrived(line[c])
        im[c, me, yl, gz] = plus(s2[c, part(gz, share)], lambda k: r2[c, k], nz - 1)
        here = im.at[c, me, yl, gz]
        line_back.append(exchange("z", lambda p: here, lambda k: here))
    for q in range(quarters):
        arrived(gram_two[q])
        gs[q] = plus(gram[q, :, part(yl, group)], lambda k: g0[q, k], nl - 1)
    flat_back = []
    for c in every:
        arrived(line_back[c])
        here = im.at[c, me, yl]
        flat_back.append(exchange("p", lambda p: here, lambda k: here))
    gram_flat = [exchange("p", lambda p: gs.at[q, p], lambda k: g1.at[q, k]) for q in range(quarters)]
    two_back = []
    for c in every:
        arrived(flat_back[c])
        here = im.at[c, :, yl]
        two_back.append(exchange("l", lambda p: here, lambda k: here))

    def full(c):
        return im[c].reshape(total, BLOCK)

    def factor(b):
        tiles = eliminate(lambda i: a_ref[TILE * i:TILE * (i + 1), :])
        for i, tile in enumerate(tiles):
            w_ref[b, TILE * i:TILE * (i + 1), :] = tile

    def projected(c):
        return dot3(split(full(c)), (xh[...], xl[...]), (0, 0))

    def finish(b):
        w = w_ref[b]
        whole = dot3(split(w), split(y_ref[b]), (1, 0))
        y_ref[b] = whole
        for s in range(species):
            core_ref[s, b * BLOCK:(b + 1) * BLOCK, :] = whole[:, s * width:(s + 1) * width]
        x = im[b, me, yl, gz]
        for a in range(b):
            x = x - hdot(basis_ref[:, a * BLOCK:(a + 1) * BLOCK], u_ref[a, b], (1, 0))
        basis_ref[:, b * BLOCK:(b + 1) * BLOCK] = hdot(x, w, (1, 1))

    for b in every:
        arrived(two_back[b])
        for a in range(b):
            raw = hdot(full(a), full(b), (0, 0))
            for d in range(a):
                raw = raw - hdot(u_ref[d, a], u_ref[d, b], (0, 0))
            u_ref[a, b] = hdot(w_ref[a], raw, (1, 0))
        raw = hdot(full(b), full(b), (0, 0))
        for d in range(b):
            raw = raw - hdot(u_ref[d, b], u_ref[d, b], (0, 0))
        a_ref[...] = raw
        y = projected(b)
        for a in range(b):
            y = y - dot3(split(u_ref[a, b]), split(y_ref[a]), (0, 0))
        y_ref[b] = y
        factor(b)
        finish(b)
        if b == 0:
            gram_line = []
            for q in range(quarters):
                arrived(gram_flat[q])
                gt[q] = plus(gs[q, me], lambda k: g1[q, k], plane - 1)
                gram_line.append(exchange("z", lambda p: gt.at[q, part(p, share)], lambda k: g2.at[q, k]))
    for q in range(quarters):
        arrived(gram_line[q])
        gram_ref[:, q * gram_width:(q + 1) * gram_width] = plus(
            gt[q, part(gz, share)], lambda k: g2[q, k], nz - 1)
    for copy in started:
        copy.wait_send()


def write_kernel(*refs):
    count = len(refs) // 2
    sems = refs[-1]
    copies = [pltpu.make_async_copy(refs[i], refs[count + i], sems.at[i]) for i in range(count)]
    for copy in copies:
        copy.start()
    for copy in copies:
        copy.wait()


def write(*arrays):
    return pl.pallas_call(
        write_kernel,
        out_shape=tuple(jax.ShapeDtypeStruct(a.shape, a.dtype) for a in arrays),
        in_specs=[pl.BlockSpec(memory_space=pltpu.VMEM)] * len(arrays),
        out_specs=(pl.BlockSpec(memory_space=pltpu.HBM),) * len(arrays),
        scratch_shapes=[pltpu.SemaphoreType.DMA((len(arrays),))],
        name="write",
    )(*arrays)


def per_device(snapshot, species_pick, basis_start):
    nx, ny, nz = lax.axis_size("gx"), lax.axis_size("gy"), lax.axis_size("gz")
    nl = 2 if ny % 2 == 0 else 1
    nh = ny // nl
    plane = nx * nh
    devices = nx * ny * nz
    stored, rows, ys, width = snapshot.shape
    species = species_pick.shape[0]
    total, rank = basis_start.shape
    share = total // devices
    group = nz * share
    blocks = rank // BLOCK
    quarters = total // rows
    chunks = chunked(species)
    scaling = 1.0 / (species * width * devices)
    most = max(len(members) for members in chunks) * width
    copies = ((len(chunks) + 2 * blocks + quarters) * (nz - 1)
              + (2 * blocks + quarters) * (plane - 1) + (2 * blocks + quarters) * (nl - 1))

    def held(*size):
        return pltpu.VMEM(size, F32)

    def half(*size):
        return pltpu.VMEM(size, BF16)

    vmem = pl.BlockSpec(memory_space=pltpu.VMEM)
    hbm = pl.BlockSpec(memory_space=pltpu.HBM)
    gram, basis, core = pl.pallas_call(
        functools.partial(main_kernel, (nx, nh, nl, nz), scaling),
        out_shape=(
            jax.ShapeDtypeStruct((share, total), F32),
            jax.ShapeDtypeStruct((share, rank), F32),
            jax.ShapeDtypeStruct((species, rank, width), F32),
        ),
        in_specs=[pl.BlockSpec(memory_space=pltpu.SMEM), hbm, hbm],
        out_specs=(vmem,) * 3,
        scratch_shapes=[
            held(stored, rows * ys, width),
            held(nz, species, rows, width),
            held(species, nz, rows, width),
            held(total, rank),
            half(total, species * width), half(total, species * width),
            half(total, rank), half(total, rank),
            half(most, rank), half(most, rank),
            held(quarters, plane, nl * group, rows),
            held(blocks, plane, nl * group, BLOCK),
            held(blocks, max(nl - 1, 1), plane, group, BLOCK),
            held(blocks, plane, group, BLOCK),
            held(blocks, max(plane - 1, 1), group, BLOCK),
            held(blocks, group, BLOCK),
            held(blocks, max(nz - 1, 1), share, BLOCK),
            held(blocks, plane, nl, nz, share, BLOCK),
            held(quarters, max(nl - 1, 1), plane, group, rows),
            held(quarters, plane, group, rows),
            held(quarters, max(plane - 1, 1), group, rows),
            held(quarters, group, rows),
            held(quarters, max(nz - 1, 1), share, rows),
            held(BLOCK, BLOCK),
            held(blocks, BLOCK, BLOCK),
            held(blocks, blocks, BLOCK, BLOCK),
            held(blocks, BLOCK, species * width),
            pltpu.SemaphoreType.DMA((stored + 1,)),
            pltpu.SemaphoreType.DMA((len(chunks),)),
            pltpu.SemaphoreType.DMA((copies,)),
            pltpu.SemaphoreType.DMA((copies,)),
        ],
        compiler_params=pltpu.CompilerParams(
            collective_id=0, has_side_effects=True, vmem_limit_bytes=56 * 2**20),
        name="main",
    )(species_pick, snapshot.reshape(stored, rows * ys, width), basis_start)
    gram, basis, core = write(gram, basis, core)
    return gram, basis, core[:, :, None, :]


def solution(mesh):
    return jax.shard_map(
        per_device,
        mesh=mesh,
        in_specs=(P(None, "gz", "gx", "gy"), P(), P()),
        out_specs=(
            P(("gx", "gy", "gz"), None),
            P(("gx", "gy", "gz"), None),
            P(None, None, ("gx", "gz"), "gy"),
        ),
        check_vma=False,
    )
```

```python
import functools

import jax
import jax.numpy as jnp
from jax import lax
from jax.experimental import pallas as pl
from jax.experimental.pallas import tpu as pltpu
from jax.sharding import PartitionSpec as P

HIGHEST = lax.Precision.HIGHEST
F32 = jnp.float32
BF16 = jnp.bfloat16
BLOCK = 128
TILE = 8
AFTER = 11
LATE = 10
HOOKS = ((0, 8), (0, 15), (0, 15), (1, 6))


def split(x):
    high = x.astype(BF16)
    return high, (x - high.astype(F32)).astype(BF16)


def dot(a, b, contract, precision=None):
    return lax.dot_general(
        a, b, (((contract[0],), (contract[1],)), ((), ())),
        precision=precision, preferred_element_type=F32,
    )


def eliminate(read, hook=None):
    count = BLOCK // TILE
    row = lax.broadcasted_iota(jnp.int32, (TILE, BLOCK), 0)
    lane = lax.broadcasted_iota(jnp.int32, (TILE, BLOCK), 1)
    left = [read(i) for i in range(count)]
    right = [(lane == row + TILE * i).astype(F32) for i in range(count)]

    def wide(x):
        return jnp.broadcast_to(x, (TILE, BLOCK))

    for t in range(count):
        if hook is not None:
            hook(t)
        columns = [wide(left[t][:, TILE * t + l:TILE * t + l + 1]) for l in range(TILE)]
        pivots, inverses, upper, lrows, rrows = [], [], [], [], []
        for l in range(TILE):
            pivot = wide(columns[l][l:l + 1, :])
            inverse = 1.0 / pivot
            factor = jnp.where(row > l, columns[l] * inverse, 0.0)
            lrow, rrow = wide(left[t][l:l + 1, :]), wide(right[t][l:l + 1, :])
            ahead = {}
            for m in range(l + 1, TILE):
                ahead[m] = wide(columns[m][l:l + 1, :])
                columns[m] = columns[m] - factor * ahead[m]
            left[t] = left[t] - factor * lrow
            right[t] = right[t] - factor * rrow
            pivots.append(pivot)
            inverses.append(inverse)
            upper.append(ahead)
            lrows.append(lrow)
            rrows.append(rrow)
        for i in range(t + 1, count):
            below = [wide(left[i][:, TILE * t + l:TILE * t + l + 1]) for l in range(TILE)]
            for l in range(TILE):
                factor = below[l] * inverses[l]
                for m in range(l + 1, TILE):
                    below[m] = below[m] - factor * upper[l][m]
                left[i] = left[i] - factor * lrows[l]
                right[i] = right[i] - factor * rrows[l]
        diagonal = pivots[0]
        for l in range(1, TILE):
            diagonal = jnp.where(row == l, pivots[l], diagonal)
        scale = lax.rsqrt(diagonal)
        scale = scale * (1.5 - 0.5 * diagonal * scale * scale)
        right[t] = right[t] * scale
    return right


def hdot(a, b, contract):
    return dot(a, b, contract, HIGHEST)


def dot3(a, b, contract):
    (ah, al), (bh, bl) = a, b
    return dot(ah, bh, contract) + (dot(ah, bl, contract) + dot(al, bh, contract))


def chunked(species):
    sizes = [2] * ((species - 2) // 2) + [1] * (species - (species - 2) // 2 * 2)
    chunks, first = [], 0
    for size in sizes:
        chunks.append(range(first, first + size))
        first += size
    return chunks


def main_kernel(dims, scaling, pick_ref, snap_ref, start_ref, gram_ref, basis_ref, core_ref,
                snap, outgoing, panel, start, xh, xl, bh, bl, wh, wl, gram, image,
                r0, s1, r1, s2, r2, im, g0, gs, gx1, gh1, gt, gx2, gh2, gu, gv, g2, a_ref, w_ref, u_ref, y_ref,
                load_sem, own_sem, send, recv):
    nx, nh, nl, nz = dims
    plane = nx * nh
    gx, gy, gz = lax.axis_index("gx"), lax.axis_index("gy"), lax.axis_index("gz")
    yh, yl = gy // nl, gy % nl
    me = gx * nh + yh
    stored = snap.shape[0]
    _, species, rows, width = outgoing.shape
    total, rank = start.shape
    blocks = rank // BLOCK
    quarters, gram_width = gram.shape[0], gram.shape[3]
    share = im.shape[4]
    group = nz * share
    tall = rows // (nl * group)
    chunks = chunked(species)
    peers = {
        "p": [(p, {"gx": p // nh, "gy": p % nh * nl + yl})
              for p in [(me + k) % plane for k in range(1, plane)]],
        "l": [(p, {"gy": yh * nl + p}) for p in [(yl + k) % nl for k in range(1, nl)]],
        "x": [(p, {"gx": p}) for p in [(gx + k) % nx for k in range(1, nx)]],
        "h": [(p, {"gy": p * nl + yl}) for p in [(yh + k) % nh for k in range(1, nh)]],
        "z": [(p, {"gz": p}) for p in [(gz + k) % nz for k in range(1, nz)]],
    }
    started = []

    def exchange(key, source, target):
        copies = []
        for k, (p, place) in enumerate(peers[key]):
            i = len(started)
            copy = pltpu.make_async_remote_copy(
                src_ref=source(p), dst_ref=target(k), send_sem=send.at[i], recv_sem=recv.at[i],
                device_id=place, device_id_type=pl.DeviceIdType.MESH,
            )
            copy.start()
            copies.append(copy)
            started.append(copy)
        return copies

    def arrived(copies):
        for copy in copies:
            copy.wait_recv()

    def part(p, size):
        return pl.ds(pl.multiple_of(p * size, size), size)

    def plus(first, buffer, count):
        for k in range(count):
            first = first + buffer(k)
        return first

    loads = [pltpu.make_async_copy(snap_ref.at[s], snap.at[s], load_sem.at[s]) for s in range(stored)]
    loads.append(pltpu.make_async_copy(start_ref, start, load_sem.at[stored]))
    for load in loads:
        load.start()
    barrier = pltpu.get_barrier_semaphore()
    count = 0
    for key in "zpl":
        for p, place in peers[key]:
            pl.semaphore_signal(barrier, inc=1, device_id=place, device_id_type=pl.DeviceIdType.MESH)
            count += 1
    for load in loads[:-1]:
        load.wait()

    landing = []
    for j, members in enumerate(chunks):
        for s in members:
            for p in range(nz):
                outgoing[p, s] = snap[pick_ref[s], pl.ds(p, rows, stride=nz), :]
        if j == 0:
            pl.semaphore_wait(barrier, count)
        these = pl.ds(members[0], len(members))
        copies = exchange("z", lambda p: outgoing.at[p, these], lambda k: panel.at[these, gz])
        own = pltpu.make_async_copy(outgoing.at[gz, these], panel.at[these, gz], own_sem.at[j])
        own.start()
        landing.append((copies, own))

    loads[-1].wait()
    bh[...], bl[...] = split(start[...])

    def columns(members):
        return slice(members[0] * width, (members[-1] + 1) * width)

    def weigh(j, members):
        copies, own = landing[j]
        own.wait()
        arrived(copies)
        for s in members:
            upper, lower = split(panel[s].reshape(total, width))
            xh[:, s * width:(s + 1) * width] = upper
            xl[:, s * width:(s + 1) * width] = lower
        cut = columns(members)
        n = len(members) * width
        w = dot3((xh[:, cut], xl[:, cut]), (bh[...], bl[...]), (0, 0)) * scaling
        wh[0:n, :], wl[0:n, :] = split(w)
        return cut

    def add_image(j, members):
        cut = weigh(j, members)
        n = len(members) * width

        @pl.loop(0, total // rows)
        def _(a):
            here = part(a, rows)
            term = dot3((xh[here, cut], xl[here, cut]), (wh[0:n, :], wl[0:n, :]), (1, 0))
            there = pl.ds(a * tall, tall)
            for c in range(blocks):
                block = term[:, c * BLOCK:(c + 1) * BLOCK].reshape(tall, nl * group, BLOCK)
                image[c, there] = block if j == 0 else image[c, there] + block

    def add_last(j, members):
        cut = weigh(j, members)
        n = len(members) * width
        sent = []
        for c in range(blocks):
            block = slice(c * BLOCK, (c + 1) * BLOCK)

            @pl.loop(0, total // rows)
            def _(a):
                here = part(a, rows)
                term = dot3((xh[here, cut], xl[here, cut]), (wh[0:n, block], wl[0:n, block]), (1, 0))
                there = pl.ds(a * tall, tall)
                image[c, there] = image[c, there] + term.reshape(tall, nl * group, BLOCK)

            sent.append(exchange("l", lambda p: image.at[c, :, part(p, group)], lambda k: r0.at[c, k]))
        return sent

    def add_gram(j, members):
        cut = columns(members)

        @pl.loop(0, total // rows)
        def _(a):
            here = part(a, rows)
            there = pl.ds(a * tall, tall)
            ah, al = xh[here, cut], xl[here, cut]
            for b in range(quarters):
                that = slice(b * gram_width, (b + 1) * gram_width)
                term = dot3((ah, al), (xh[that, cut], xl[that, cut]), (1, 1))
                term = term.reshape(tall, nl * group, gram_width)
                if j > 0:
                    term = term + gram[b, there]
                if j == len(chunks) - 1:
                    term = term * scaling
                gram[b, there] = term

    every = range(blocks)
    for j, members in enumerate(chunks[:-1]):
        add_image(j, members)
        add_gram(j, members)
    two = add_last(len(chunks) - 1, chunks[-1])

    def to_plane(c):
        arrived(two[c])
        s1[c] = plus(image[c, :, part(yl, group)], lambda k: r0[c, k], nl - 1)
        return exchange("p", lambda p: s1.at[c, p], lambda k: r1.at[c, k])

    def to_line(c):
        arrived(flat[c])
        s2[c] = plus(s1[c, me], lambda k: r1[c, k], plane - 1)
        return exchange("z", lambda p: s2.at[c, part(p, share)], lambda k: r2.at[c, k])

    def from_line(c):
        arrived(line[c])
        im[c, me, yl, gz] = plus(s2[c, part(gz, share)], lambda k: r2[c, k], nz - 1)
        here = im.at[c, me, yl, gz]
        return exchange("z", lambda p: here, lambda k: here)

    def from_plane(c):
        arrived(line_back[c])
        here = im.at[c, me, yl]
        return exchange("p", lambda p: here, lambda k: here)

    def from_two(c):
        arrived(flat_back[c])
        here = im.at[c, :, yl]
        return exchange("l", lambda p: here, lambda k: here)

    def gram_pair(q):
        arrived(gram_two[q])
        for m in range(plane):
            gs[q, m // nh, m % nh] = plus(gram[q, m, part(yl, group)], lambda k: g0[q, k, m], nl - 1)

    def gram_first(q):
        if q % 2 == 0:
            return exchange("x", lambda p: gs.at[q, p], lambda k: gx1.at[q // 2, k])
        return exchange("h", lambda p: gs.at[q, :, p], lambda k: gh1.at[q // 2, k])

    def gram_second(q):
        arrived(gram_half[q])
        if q % 2 == 0:
            gt[q // 2] = plus(gs[q, gx], lambda k: gx1[q // 2, k], nx - 1)
            return exchange("h", lambda p: gt.at[q // 2, p], lambda k: gh2.at[q // 2, k])
        gu[q // 2] = plus(gs[q, :, yh], lambda k: gh1[q // 2, k], nh - 1)
        return exchange("x", lambda p: gu.at[q // 2, p], lambda k: gx2.at[q // 2, k])

    def gram_third(q):
        arrived(gram_whole[q])
        if q % 2 == 0:
            whole = plus(gt[q // 2, yh], lambda k: gh2[q // 2, k], nh - 1)
        else:
            whole = plus(gu[q // 2, gx], lambda k: gx2[q // 2, k], nx - 1)
        gv[q] = whole
        return exchange("z", lambda p: gv.at[q, part(p, share)], lambda k: g2.at[q, k])

    def gram_last(q):
        arrived(gram_line[q])
        gram_ref[:, q * gram_width:(q + 1) * gram_width] = plus(
            gv[q, part(gz, share)], lambda k: g2[q, k], nz - 1)

    flat, line, line_back, flat_back, two_back = {}, {}, {}, {}, {}
    gram_two, gram_half, gram_whole, gram_line = {}, {}, {}, {}
    for c in every:
        flat[c] = to_plane(c)
    add_gram(len(chunks) - 1, chunks[-1])
    for q in range(quarters):
        gram_two[q] = exchange("l", lambda p: gram.at[q, :, part(p, group)], lambda k: g0.at[q, k])
    early, late = range(quarters // 2), range(quarters // 2, quarters)
    steps = sorted(
        [(2 * c, c, line, to_line) for c in every]
        + [(2 * c + 3, c, line_back, from_line) for c in every]
        + [(2 * c + 6, c, flat_back, from_plane) for c in every]
        + [(AFTER, 0, two_back, from_two)],
        key=lambda step: step[0],
    )
    for order, c, into, step in steps:
        into[c] = step(c)
        if order == 2:
            for q in range(quarters):
                gram_pair(q)
            for q in early:
                gram_half[q] = gram_first(q)
        if order == LATE:
            for q in late:
                gram_half[q] = gram_first(q)


    def during(b, t):
        if (b, t) == HOOKS[0]:
            for c in range(1, blocks):
                two_back[c] = from_two(c)
            for q in early:
                gram_whole[q] = gram_second(q)
        if (b, t) == HOOKS[1]:
            for q in early:
                gram_line[q] = gram_third(q)
        if (b, t) == HOOKS[2]:
            for q in late:
                gram_whole[q] = gram_second(q)
        if (b, t) == HOOKS[3]:
            for q in late:
                gram_line[q] = gram_third(q)

    def full(c):
        return im[c].reshape(total, BLOCK)

    def factor(b):
        tiles = eliminate(lambda i: a_ref[TILE * i:TILE * (i + 1), :], functools.partial(during, b))
        for i, tile in enumerate(tiles):
            w_ref[b, TILE * i:TILE * (i + 1), :] = tile

    def projected(c):
        return dot3(split(full(c)), (xh[...], xl[...]), (0, 0))

    def finish(b):
        w = w_ref[b]
        whole = dot3(split(w), split(y_ref[b]), (1, 0))
        y_ref[b] = whole
        for s in range(species):
            core_ref[s, b * BLOCK:(b + 1) * BLOCK, :] = whole[:, s * width:(s + 1) * width]
        x = im[b, me, yl, gz]
        for a in range(b):
            x = x - hdot(basis_ref[:, a * BLOCK:(a + 1) * BLOCK], u_ref[a, b], (1, 0))
        basis_ref[:, b * BLOCK:(b + 1) * BLOCK] = hdot(x, w, (1, 1))

    for b in every:
        arrived(two_back[b])
        for a in range(b):
            raw = hdot(full(a), full(b), (0, 0))
            for d in range(a):
                raw = raw - hdot(u_ref[d, a], u_ref[d, b], (0, 0))
            u_ref[a, b] = hdot(w_ref[a], raw, (1, 0))
        raw = hdot(full(b), full(b), (0, 0))
        for d in range(b):
            raw = raw - hdot(u_ref[d, b], u_ref[d, b], (0, 0))
        a_ref[...] = raw
        y = projected(b)
        for a in range(b):
            y = y - dot3(split(u_ref[a, b]), split(y_ref[a]), (0, 0))
        y_ref[b] = y
        factor(b)
        finish(b)
    for q in range(quarters):
        gram_last(q)
    for copy in started:
        copy.wait_send()


def write_kernel(*refs):
    count = len(refs) // 2
    sems = refs[-1]
    copies = [pltpu.make_async_copy(refs[i], refs[count + i], sems.at[i]) for i in range(count)]
    for copy in copies:
        copy.start()
    for copy in copies:
        copy.wait()


def write(*arrays):
    return pl.pallas_call(
        write_kernel,
        out_shape=tuple(jax.ShapeDtypeStruct(a.shape, a.dtype) for a in arrays),
        in_specs=[pl.BlockSpec(memory_space=pltpu.VMEM)] * len(arrays),
        out_specs=(pl.BlockSpec(memory_space=pltpu.HBM),) * len(arrays),
        scratch_shapes=[pltpu.SemaphoreType.DMA((len(arrays),))],
        compiler_params=pltpu.CompilerParams(vmem_limit_bytes=4 * 2**20),
        name="write",
    )(*arrays)


def per_device(snapshot, species_pick, basis_start):
    nx, ny, nz = lax.axis_size("gx"), lax.axis_size("gy"), lax.axis_size("gz")
    nl = 2 if ny % 2 == 0 else 1
    nh = ny // nl
    plane = nx * nh
    devices = nx * ny * nz
    stored, rows, ys, width = snapshot.shape
    species = species_pick.shape[0]
    total, rank = basis_start.shape
    share = total // devices
    group = nz * share
    blocks = rank // BLOCK
    quarters = total // rows
    chunks = chunked(species)
    scaling = 1.0 / (species * width * devices)
    most = max(len(members) for members in chunks) * width
    copies = ((len(chunks) + 2 * blocks + quarters) * (nz - 1)
              + 2 * blocks * (plane - 1) + quarters * (nx - 1 + nh - 1) + (2 * blocks + quarters) * (nl - 1))

    def held(*size):
        return pltpu.VMEM(size, F32)

    def half(*size):
        return pltpu.VMEM(size, BF16)

    vmem = pl.BlockSpec(memory_space=pltpu.VMEM)
    hbm = pl.BlockSpec(memory_space=pltpu.HBM)
    gram, basis, core = pl.pallas_call(
        functools.partial(main_kernel, (nx, nh, nl, nz), scaling),
        out_shape=(
            jax.ShapeDtypeStruct((share, total), F32),
            jax.ShapeDtypeStruct((share, rank), F32),
            jax.ShapeDtypeStruct((species, rank, width), F32),
        ),
        in_specs=[pl.BlockSpec(memory_space=pltpu.SMEM), hbm, hbm],
        out_specs=(vmem,) * 3,
        scratch_shapes=[
            held(stored, rows * ys, width),
            held(nz, species, rows, width),
            held(species, nz, rows, width),
            held(total, rank),
            half(total, species * width), half(total, species * width),
            half(total, rank), half(total, rank),
            half(most, rank), half(most, rank),
            held(quarters, plane, nl * group, rows),
            held(blocks, plane, nl * group, BLOCK),
            held(blocks, max(nl - 1, 1), plane, group, BLOCK),
            held(blocks, plane, group, BLOCK),
            held(blocks, max(plane - 1, 1), group, BLOCK),
            held(blocks, group, BLOCK),
            held(blocks, max(nz - 1, 1), share, BLOCK),
            held(blocks, plane, nl, nz, share, BLOCK),
            held(quarters, max(nl - 1, 1), plane, group, rows),
            held(quarters, nx, nh, group, rows),
            held(quarters // 2, max(nx - 1, 1), nh, group, rows),
            held(quarters // 2, max(nh - 1, 1), nx, group, rows),
            held(quarters // 2, nh, group, rows),
            held(quarters // 2, max(nx - 1, 1), group, rows),
            held(quarters // 2, max(nh - 1, 1), group, rows),
            held(quarters // 2, nx, group, rows),
            held(quarters, group, rows),
            held(quarters, max(nz - 1, 1), share, rows),
            held(BLOCK, BLOCK),
            held(blocks, BLOCK, BLOCK),
            held(blocks, blocks, BLOCK, BLOCK),
            held(blocks, BLOCK, species * width),
            pltpu.SemaphoreType.DMA((stored + 1,)),
            pltpu.SemaphoreType.DMA((len(chunks),)),
            pltpu.SemaphoreType.DMA((copies,)),
            pltpu.SemaphoreType.DMA((copies,)),
        ],
        compiler_params=pltpu.CompilerParams(
            collective_id=0, has_side_effects=True, vmem_limit_bytes=52 * 2**20),
        name="main",
    )(species_pick, snapshot.reshape(stored, rows * ys, width), basis_start)
    gram, basis, core = write(gram, basis, core)
    return gram, basis, core[:, :, None, :]


def solution(mesh):
    return jax.shard_map(
        per_device,
        mesh=mesh,
        in_specs=(P(None, "gz", "gx", "gy"), P(), P()),
        out_specs=(
            P(("gx", "gy", "gz"), None),
            P(("gx", "gy", "gz"), None),
            P(None, None, ("gx", "gz"), "gy"),
        ),
        check_vma=False,
    )
```
